32 devices in a mesh: parts: 2 (over x), col: 16 (over z, y, core).
Axes of the slice: x: 2, y: 2, z: 4, core: 2. Of those that a mesh axis runs over, the one named last changes fastest.
Arguments:
- view_factors: bfloat16 [8192, 4096], P(('parts', 'col')), parts along dimension 0, may hold values from -0.09375 to 0.09375
- direct_coeff: bfloat16 [8192, 2304], P(('parts', 'col')), parts along dimension 0, may hold values from -6 to 6
- material: int32 [8192], P(('parts', 'col')), parts along dimension 0, may hold values from 0 to 15
- albedo: float32 [32], P('parts'), parts along dimension 0, may hold values from 0.1 to 0.9
- sky_matrix: bfloat16 [2304, 128], P('col'), may hold values from -0.125 to 0.125
- sky_order: int32 [2304], replicated, may hold values from 0 to 2303, each once
Outputs:
- irradiance: bfloat16 [8192, 128], P(('parts', 'col')), parts along dimension 0
The draws below stay inside these ranges and needn't reach their ends.
There are 2 independent parts, one for each index of `parts`. The reference program is written for one: setup_inputs(seed, part) draws one part's arguments, and reference() takes and returns one part's arrays. A program takes and returns all parts, laid end to end along the dimension named above; an argument that names none is the same for every part. Nothing has to cross between parts.
Inputs may be any that keep to these rules, and one draw needn't show every extreme that they name: sky_order names each of 0 to 2303 once.
All inputs are finite; a program needn't handle non-finite values.
Results may differ from the reference program's by a relative error of at most 0.0055.
Values may be sent and summed in bfloat16 or wider, within the bound.
A program may use at most 128 MiB of HBM per device.

```python
import jax
import jax.numpy as jnp
from jax import lax

SKY = 2304
MATERIALS = 16
HOURS = 128
PATCHES = 4096


def set_ends(values, stream_key, smallest, largest):
    longest = values.shape.index(max(values.shape))
    spots = []
    for shift in (0, 1):
        where = [jax.random.randint(jax.random.fold_in(stream_key, axis), (), 0, length) for axis, length in enumerate(values.shape)]
        where[longest] = (where[longest] + shift) % values.shape[longest]
        spots.append(tuple(where))
    return values.at[spots[0]].set(smallest).at[spots[1]].set(largest)


def block_levels(rng, extent, cuts, least, largest):
    loudness = 1.0
    for dim, blocks in cuts:
        heights = jax.random.uniform(jax.random.fold_in(jax.random.fold_in(rng, 6), dim), (blocks,), jnp.float32, least / len(cuts), largest / len(cuts))
        loudness = loudness * jnp.repeat(jnp.exp(heights), extent[dim] // blocks).reshape((-1,) + (1,) * (len(extent) - 1 - dim))
    return loudness


def gaussian(rng, extent, width, bound, cuts=(), held_as=jnp.bfloat16):
    factor_of = block_levels(rng, extent, cuts, -0.22, 0.18) if cuts else 1.0
    result = jax.random.normal(rng, extent, jnp.float32) * width * factor_of
    return jnp.minimum(jnp.maximum(result, -bound), bound).astype(held_as)


def setup_inputs(seed: int = 0, part: int = 0) -> dict:
    seeds = jax.random.split(jax.random.key(seed), 7)
    part_keys = jax.random.split(jax.random.fold_in(seeds[6], part), 7)
    return {
        "view_factors": gaussian(part_keys[0], (PATCHES, PATCHES), PATCHES ** -0.5, 0.09375, ((0, 16),)),
        "direct_coeff": gaussian(part_keys[1], (PATCHES, SKY), 1.0, 6.0, ((0, 16),)),
        "material": set_ends(jax.random.randint(part_keys[2], (PATCHES,), 0, MATERIALS), jax.random.fold_in(part_keys[2], 1), 0, MATERIALS - 1).astype(jnp.int32),
        "albedo": jnp.clip(jax.random.uniform(part_keys[3], (MATERIALS,), jnp.float32, 0.1, 0.9), 0.1, 0.9),
        "sky_matrix": gaussian(seeds[4], (SKY, HOURS), SKY ** -0.5, 0.125, ((0, 16),)),
        "sky_order": jax.random.permutation(seeds[5], SKY).astype(jnp.int32),
    }


def reference(view_factors, direct_coeff, material, albedo, sky_matrix, sky_order):
    reflectance = albedo[material]
    reflected = (reflectance[:, None] * direct_coeff.astype(jnp.float32)).astype(jnp.bfloat16)
    bounce = jnp.dot(view_factors, reflected, preferred_element_type=jnp.float32)
    coefficients = direct_coeff.astype(jnp.float32) + bounce
    ordered = sky_matrix[sky_order.astype(jnp.int32)]
    irradiance = jnp.dot(coefficients, ordered.astype(jnp.float32), precision=lax.Precision.HIGHEST)
    return irradiance.astype(jnp.bfloat16)
```

```python
import functools

import jax
import jax.numpy as jnp
from jax import lax
from jax.experimental import pallas as pl
from jax.experimental.pallas import tpu as pltpu
from jax.sharding import PartitionSpec as P

MESH = pl.DeviceIdType.MESH
LANES = 128
WIDE = 256
BF16 = jnp.bfloat16
F32 = jnp.float32


def partner(index, step, count):
    if count & (count - 1):
        return lax.rem(index + step, count)
    result, bit = 0, 1
    while bit < count:
        digit = lax.rem(lax.div(index, bit), 2)
        if step & bit:
            digit = 1 - digit
        result = result + digit * bit
        bit *= 2
    return result


def kernel(
    dims,
    view_hbm,
    direct_hbm,
    material_ref,
    albedo_ref,
    sky_hbm,
    place_ref,
    out_ref,
    view_ref,
    direct_ref,
    sky_all,
    hours_all,
    low_ref,
    high_ref,
    reflectance_ref,
    sorted_ref,
    reflected_ref,
    load_sem,
    send_sem,
    recv_sem,
):
    nz, ny, nc = dims
    me = lax.axis_index("col")
    c = lax.rem(me, nc)
    y = lax.rem(lax.div(me, nc), ny)
    z = lax.div(me, nc * ny)

    def index(zz, yy, cc):
        return (zz * ny + yy) * nc + cc

    zs = [partner(z, d, nz) for d in range(nz)]
    zs[0] = z
    line = [index(zz, y, c) for zz in zs[1:]]
    across = index(z, 1 - y, c) if ny == 2 else None
    twin = index(z, y, 1 - c) if nc == 2 else None
    partners = line + [p for p in (across, twin) if p is not None]

    rows = view_ref.shape[0]
    sky_rows = sky_hbm.shape[0]
    own_sky = sky_all.at[pl.ds(pl.multiple_of(me * sky_rows, 16), sky_rows), :]

    load_sky = pltpu.make_async_copy(sky_hbm, own_sky, load_sem.at[0])
    load_direct = pltpu.make_async_copy(direct_hbm, direct_ref, load_sem.at[1])
    load_view = pltpu.make_async_copy(view_hbm, view_ref, load_sem.at[2])
    load_sky.start()
    load_direct.start()
    load_view.start()

    barrier = pltpu.get_barrier_semaphore()
    for p in partners:
        pl.semaphore_signal(barrier, inc=1, device_id={"col": p}, device_id_type=MESH)

    lane = lax.broadcasted_iota(jnp.int32, (LANES, LANES), 1)
    for b in range(place_ref.shape[0]):
        spot = jnp.broadcast_to(place_ref[b : b + 1, :], (LANES, LANES)).T
        low = jnp.where(lax.bitwise_and(spot, LANES - 1) == lane, 1.0, 0.0)
        low_ref[b * LANES : (b + 1) * LANES, :] = low.astype(BF16)
        high = lax.shift_right_logical(spot, LANES.bit_length() - 1)
        high_ref[b * LANES : (b + 1) * LANES, :] = high.astype(F32).astype(BF16)
    for b in range(material_ref.shape[0]):
        kind = jnp.broadcast_to(material_ref[b : b + 1, :], (LANES, LANES)).T
        value = jnp.zeros((LANES, LANES), F32)
        for m in range(albedo_ref.shape[0]):
            value = jnp.where(kind == m, albedo_ref[m], value)
        reflectance_ref[b * LANES : (b + 1) * LANES, :] = value

    load_sky.wait()
    pl.semaphore_wait(barrier, len(partners))

    sends = []

    def send(phase, everyone, block, owner, target, route):
        part = everyone.at[pl.ds(pl.multiple_of(owner * block, 16), block), :]
        copy = pltpu.make_async_remote_copy(
            src_ref=part,
            dst_ref=part,
            send_sem=send_sem.at[phase, route],
            recv_sem=recv_sem.at[phase, owner],
            device_id={"col": target},
            device_id_type=MESH,
        )
        copy.start()
        sends.append(copy)

    def arrived(phase, everyone, block, owner):
        part = everyone.at[pl.ds(pl.multiple_of(owner * block, 16), block), :]
        pltpu.make_async_copy(part, part, recv_sem.at[phase, owner]).wait()

    def gather(phase, everyone, block, work):
        route = iter(range(2 * nz * ny * nc))
        if across is not None:
            send(phase, everyone, block, me, across, next(route))
        for p in reversed(line):
            send(phase, everyone, block, me, p, next(route))
        if twin is not None:
            send(phase, everyone, block, me, twin, next(route))
        work(me)
        waits = []
        for d in range(1, nz):
            waits.append((zs[d], y, True))
        if across is not None:
            waits.insert(0, (z, 1 - y, False))
            for d in range(1, nz):
                waits.append((zs[d], 1 - y, False))
        for zz, yy, forward in waits:
            owner = index(zz, yy, c)
            arrived(phase, everyone, block, owner)
            if forward and across is not None:
                send(phase, everyone, block, owner, across, next(route))
            if twin is not None:
                send(phase, everyone, block, owner, twin, next(route))
            work(owner)
        if twin is not None:
            for zz, yy in [(z, y)] + [(zz, yy) for zz, yy, _ in waits]:
                owner = index(zz, yy, 1 - c)
                arrived(phase, everyone, block, owner)
                work(owner)

    groups = sorted_ref.shape[1] // WIDE
    done = [False]

    def sort_columns(group):
        start = pl.multiple_of(group * WIDE, WIDE)
        halves = []
        for half in range(WIDE // LANES):
            number = (group * (WIDE // LANES) + half).astype(F32).astype(BF16)
            halves.append(jnp.where(high_ref[...] == number, low_ref[...], jnp.zeros((), BF16)))
        chosen = jnp.concatenate(halves, axis=1)
        values = jnp.dot(direct_ref[...], chosen, preferred_element_type=F32)
        sorted_ref[:, pl.ds(start, WIDE)] = values.astype(BF16)
        scale = jnp.concatenate([reflectance_ref[...]] * (WIDE // LANES), axis=1)
        reflected_ref[:, pl.ds(start, WIDE)] = (scale * values).astype(BF16)

    def sort_all(owner):
        if not done[0]:
            done[0] = True
            load_direct.wait()
            lax.fori_loop(0, groups, lambda g, _: (sort_columns(g), 0)[1], 0)

    gather(0, sky_all, sky_rows, sort_all)

    own_hours = pl.ds(pl.multiple_of(me * rows, 16), rows)
    hours_all[own_hours, :] = jnp.dot(reflected_ref[...], sky_all[...], preferred_element_type=F32).astype(BF16)

    total = [None]

    def add(owner):
        if total[0] is None:
            load_view.wait()
            total[0] = jnp.dot(sorted_ref[...], sky_all[...], preferred_element_type=F32)
        start = pl.multiple_of(owner * rows, LANES)
        total[0] = total[0] + jnp.dot(
            view_ref[:, pl.ds(start, rows)], hours_all[pl.ds(start, rows), :], preferred_element_type=F32
        )

    gather(1, hours_all, rows, add)
    out_ref[...] = total[0].astype(out_ref.dtype)
    for copy in sends:
        copy.wait_send()


def shards(dims, view_factors, direct_coeff, material, albedo, sky_matrix, sky_order):
    count = dims[0] * dims[1] * dims[2]
    rows, patches = view_factors.shape
    sky, hours = direct_coeff.shape[1], sky_matrix.shape[1]
    held = sky_matrix.shape[0]
    padded = -(-held // 16) * 16
    place = sky_order
    if padded != held:
        sky_matrix = jnp.pad(sky_matrix, ((0, padded - held), (0, 0)))
        place = sky_order // held * padded + sky_order % held
    width = -(-count * padded // WIDE) * WIDE
    assert width == count * padded and sky % LANES == 0
    routes = 2 * count
    any_spec = pl.BlockSpec(memory_space=pl.ANY)
    vmem = pl.BlockSpec(memory_space=pltpu.VMEM)
    smem = pl.BlockSpec(memory_space=pltpu.SMEM)
    return pl.pallas_call(
        functools.partial(kernel, dims),
        out_shape=jax.ShapeDtypeStruct((rows, hours), BF16),
        in_specs=[any_spec, any_spec, vmem, smem, any_spec, vmem],
        out_specs=vmem,
        scratch_shapes=[
            pltpu.VMEM((rows, patches), BF16),
            pltpu.VMEM((rows, sky), BF16),
            pltpu.VMEM((width, hours), BF16),
            pltpu.VMEM((patches, hours), BF16),
            pltpu.VMEM((sky, LANES), BF16),
            pltpu.VMEM((sky, LANES), BF16),
            pltpu.VMEM((rows, LANES), F32),
            pltpu.VMEM((rows, width), BF16),
            pltpu.VMEM((rows, width), BF16),
            pltpu.SemaphoreType.DMA((3,)),
            pltpu.SemaphoreType.DMA((2, routes)),
            pltpu.SemaphoreType.DMA((2, count)),
        ],
        compiler_params=pltpu.CompilerParams(
            collective_id=0, has_side_effects=True, vmem_limit_bytes=60 * 2**20
        ),
    )(
        view_factors,
        direct_coeff,
        material.reshape(-1, LANES),
        albedo,
        sky_matrix,
        place.reshape(-1, LANES),
    )


def solution(mesh):
    count, parts = mesh.shape["col"], mesh.shape["parts"]
    cores = 2 if count % 2 == 0 else 1
    side = 2 if parts <= 2 and count % (2 * cores) == 0 else 1
    dims = (count // (side * cores), side, cores)
    return jax.shard_map(
        functools.partial(shards, dims),
        mesh=mesh,
        in_specs=(
            P(("parts", "col"), None),
            P(("parts", "col"), None),
            P(("parts", "col")),
            P("parts"),
            P("col", None),
            P(),
        ),
        out_specs=P(("parts", "col"), None),
        check_vma=False,
    )
```

```python
import functools

import jax
import jax.numpy as jnp
from jax import lax
from jax.experimental import pallas as pl
from jax.experimental.pallas import tpu as pltpu
from jax.sharding import PartitionSpec as P

MESH = pl.DeviceIdType.MESH
LANES = 128
WIDE = 256
STAGES = (9,)
BF16 = jnp.bfloat16
F32 = jnp.float32


def partner(index, step, count):
    if count & (count - 1):
        return lax.rem(index + step, count)
    result, bit = 0, 1
    while bit < count:
        digit = lax.rem(lax.div(index, bit), 2)
        if step & bit:
            digit = 1 - digit
        result = result + digit * bit
        bit *= 2
    return result


def kernel(
    dims,
    view_hbm,
    direct_hbm,
    material_hbm,
    albedo_hbm,
    sky_hbm,
    place_hbm,
    out_ref,
    view_ref,
    direct_ref,
    sky_all,
    hours_all,
    low_ref,
    high_ref,
    reflectance_ref,
    sorted_ref,
    reflected_ref,
    material_ref,
    albedo_ref,
    place_ref,
    load_sem,
    send_sem,
    recv_sem,
):
    nz, ny, nc = dims
    me = lax.axis_index("col")
    c = lax.rem(me, nc)
    y = lax.rem(lax.div(me, nc), ny)
    z = lax.div(me, nc * ny)

    def index(zz, yy, cc):
        return (zz * ny + yy) * nc + cc

    zs = [partner(z, d, nz) for d in range(nz)]
    zs[0] = z
    line = [index(zz, y, c) for zz in zs[1:]]
    across = index(z, 1 - y, c) if ny == 2 else None
    twin = index(z, y, 1 - c) if nc == 2 else None
    partners = line + [p for p in (across, twin) if p is not None]

    rows = view_ref.shape[0]
    sky_rows = sky_hbm.shape[0]
    own_sky = sky_all.at[pl.ds(pl.multiple_of(me * sky_rows, 16), sky_rows), :]

    load_sky = pltpu.make_async_copy(sky_hbm, own_sky, load_sem.at[0])
    load_direct = pltpu.make_async_copy(direct_hbm, direct_ref, load_sem.at[1])
    load_view = pltpu.make_async_copy(view_hbm, view_ref, load_sem.at[2])
    barrier = pltpu.get_barrier_semaphore()
    for p in partners:
        pl.semaphore_signal(barrier, inc=1, device_id={"col": p}, device_id_type=MESH)

    load_place = pltpu.make_async_copy(place_hbm, place_ref, load_sem.at[3])
    load_material = pltpu.make_async_copy(material_hbm, material_ref, load_sem.at[4])
    load_albedo = pltpu.make_async_copy(albedo_hbm, albedo_ref, load_sem.at[5])
    load_place.start()
    load_material.start()
    load_albedo.start()
    load_sky.start()
    load_direct.start()
    load_view.start()

    load_place.wait()
    lane = lax.broadcasted_iota(jnp.int32, (LANES, LANES), 1)
    for b in range(place_ref.shape[0]):
        spot = jnp.broadcast_to(place_ref[b : b + 1, :], (LANES, LANES)).T
        low = jnp.where(lax.bitwise_and(spot, LANES - 1) == lane, 1.0, 0.0)
        low_ref[b * LANES : (b + 1) * LANES, :] = low.astype(BF16)
        high = lax.shift_right_logical(spot, LANES.bit_length() - 1)
        high_ref[b * LANES : (b + 1) * LANES, :] = high.astype(F32).astype(BF16)
    load_material.wait()
    load_albedo.wait()
    for b in range(material_ref.shape[0]):
        kind = jnp.broadcast_to(material_ref[b : b + 1, :], (LANES, LANES)).T
        value = jnp.zeros((LANES, LANES), F32)
        for m in range(albedo_ref.shape[0]):
            value = jnp.where(kind == m, albedo_ref[m], value)
        reflectance_ref[b * LANES : (b + 1) * LANES, :] = value

    groups = sorted_ref.shape[1] // WIDE
    done = [0]

    def sort_columns(group):
        start = pl.multiple_of(group * WIDE, WIDE)
        halves = []
        for half in range(WIDE // LANES):
            number = (group * (WIDE // LANES) + half).astype(F32).astype(BF16)
            halves.append(jnp.where(high_ref[...] == number, low_ref[...], jnp.zeros((), BF16)))
        chosen = jnp.concatenate(halves, axis=1)
        values = jnp.dot(direct_ref[...], chosen, preferred_element_type=F32)
        sorted_ref[:, pl.ds(start, WIDE)] = values.astype(BF16)
        scale = jnp.concatenate([reflectance_ref[...]] * (WIDE // LANES), axis=1)
        reflected_ref[:, pl.ds(start, WIDE)] = (scale * values).astype(BF16)

    def sort_range(first, last):
        lax.fori_loop(first, last, lambda g, _: (sort_columns(g), 0)[1], 0)

    load_sky.wait()
    pl.semaphore_wait(barrier, len(partners))

    sends = []

    def send(phase, everyone, block, owner, target, route):
        part = everyone.at[pl.ds(pl.multiple_of(owner * block, 16), block), :]
        copy = pltpu.make_async_remote_copy(
            src_ref=part,
            dst_ref=part,
            send_sem=send_sem.at[phase, route],
            recv_sem=recv_sem.at[phase, owner],
            device_id={"col": target},
            device_id_type=MESH,
        )
        copy.start()
        sends.append(copy)

    def arrived(phase, everyone, block, owner):
        part = everyone.at[pl.ds(pl.multiple_of(owner * block, 16), block), :]
        pltpu.make_async_copy(part, part, recv_sem.at[phase, owner]).wait()

    def gather(phase, everyone, block, work):
        route = iter(range(2 * nz * ny * nc))
        if across is not None:
            send(phase, everyone, block, me, across, next(route))
        for p in line:
            send(phase, everyone, block, me, p, next(route))
        if twin is not None:
            send(phase, everyone, block, me, twin, next(route))
        work(me)
        waits = []
        for d in range(1, nz):
            waits.append((zs[d], y, True))
        if across is not None:
            waits.insert(0, (z, 1 - y, False))
            for d in range(1, nz):
                waits.append((zs[d], 1 - y, False))
        for zz, yy, forward in waits:
            owner = index(zz, yy, c)
            arrived(phase, everyone, block, owner)
            if forward and across is not None:
                send(phase, everyone, block, owner, across, next(route))
            if twin is not None:
                send(phase, everyone, block, owner, twin, next(route))
            work(owner)
        if twin is not None:
            for zz, yy in [(z, y)] + [(zz, yy) for zz, yy, _ in waits]:
                owner = index(zz, yy, 1 - c)
                arrived(phase, everyone, block, owner)
                work(owner)

    def sort_some(owner):
        step = done[0]
        if step == 0:
            load_direct.wait()
        if step < len(STAGES):
            sort_range(groups * (STAGES[step - 1] if step else 0) // 9, groups * STAGES[step] // 9)
        done[0] = step + 1

    gather(0, sky_all, sky_rows, sort_some)

    own_hours = pl.ds(pl.multiple_of(me * rows, 16), rows)
    hours_all[own_hours, :] = jnp.dot(reflected_ref[...], sky_all[...], preferred_element_type=F32).astype(BF16)

    total = [None]

    def add(owner):
        if total[0] is None:
            load_view.wait()
            total[0] = jnp.dot(sorted_ref[...], sky_all[...], preferred_element_type=F32)
        start = pl.multiple_of(owner * rows, LANES)
        total[0] = total[0] + jnp.dot(
            view_ref[:, pl.ds(start, rows)], hours_all[pl.ds(start, rows), :], preferred_element_type=F32
        )

    gather(1, hours_all, rows, add)
    out_ref[...] = total[0].astype(out_ref.dtype)
    for copy in sends:
        copy.wait_send()


def shards(dims, view_factors, direct_coeff, material, albedo, sky_matrix, sky_order):
    count = dims[0] * dims[1] * dims[2]
    rows, patches = view_factors.shape
    sky, hours = direct_coeff.shape[1], sky_matrix.shape[1]
    held = sky_matrix.shape[0]
    padded = -(-held // 16) * 16
    place = sky_order
    if padded != held:
        sky_matrix = jnp.pad(sky_matrix, ((0, padded - held), (0, 0)))
        place = sky_order // held * padded + sky_order % held
    width = -(-count * padded // WIDE) * WIDE
    assert width == count * padded and sky % LANES == 0
    routes = 2 * count
    hbm = pl.BlockSpec(memory_space=pltpu.HBM)
    vmem = pl.BlockSpec(memory_space=pltpu.VMEM)
    return pl.pallas_call(
        functools.partial(kernel, dims),
        out_shape=jax.ShapeDtypeStruct((rows, hours), BF16),
        in_specs=[hbm] * 6,
        out_specs=vmem,
        scratch_shapes=[
            pltpu.VMEM((rows, patches), BF16),
            pltpu.VMEM((rows, sky), BF16),
            pltpu.VMEM((width, hours), BF16),
            pltpu.VMEM((patches, hours), BF16),
            pltpu.VMEM((sky, LANES), BF16),
            pltpu.VMEM((sky, LANES), BF16),
            pltpu.VMEM((rows, LANES), F32),
            pltpu.VMEM((rows, width), BF16),
            pltpu.VMEM((rows, width), BF16),
            pltpu.VMEM((rows // LANES, LANES), jnp.int32),
            pltpu.SMEM(albedo.shape, F32),
            pltpu.VMEM((sky // LANES, LANES), jnp.int32),
            pltpu.SemaphoreType.DMA((6,)),
            pltpu.SemaphoreType.DMA((2, routes)),
            pltpu.SemaphoreType.DMA((2, count)),
        ],
        compiler_params=pltpu.CompilerParams(
            collective_id=0, has_side_effects=True, vmem_limit_bytes=60 * 2**20
        ),
    )(
        view_factors,
        direct_coeff,
        material.reshape(-1, LANES),
        albedo,
        sky_matrix,
        place.reshape(-1, LANES),
    )


def solution(mesh):
    count, parts = mesh.shape["col"], mesh.shape["parts"]
    cores = 2 if count % 2 == 0 else 1
    side = 2 if parts <= 2 and count % (2 * cores) == 0 else 1
    dims = (count // (side * cores), side, cores)
    return jax.shard_map(
        functools.partial(shards, dims),
        mesh=mesh,
        in_specs=(
            P(("parts", "col"), None),
            P(("parts", "col"), None),
            P(("parts", "col")),
            P("parts"),
            P("col", None),
            P(),
        ),
        out_specs=P(("parts", "col"), None),
        check_vma=False,
    )
```
